32 devices in a mesh: parts: 2 (over y), col: 4 (over z), row: 4 (over x, core).
Axes of the slice: x: 2, y: 2, z: 4, core: 2. Of those that a mesh axis runs over, the one named last changes fastest.
Arguments:
- grad_table: bfloat16 [16384, 32768], P(('parts', 'row'), 'col'), parts along dimension 0, may hold values from -60 to 60
- prev_embed: bfloat16 [8192, 512], P('row', 'col'), may hold values from -6 to 6
- next_embed: bfloat16 [32768, 512], P('col', 'row'), may hold values from -6 to 6
- log_norm: float32 [16384], P(('parts', 'row')), parts along dimension 0, may hold values from 9 to 11
Outputs:
- prev_grad: float32 [16384, 512], P(('parts', 'row'), 'col'), parts along dimension 0
- next_grad: float32 [65536, 512], P(('parts', 'col'), 'row'), parts along dimension 0
The draws below stay inside these ranges and needn't reach their ends.
There are 2 independent parts, one for each index of `parts`. The reference program is written for one: setup_inputs(seed, part) draws one part's arguments, and reference() takes and returns one part's arrays. A program takes and returns all parts, laid end to end along the dimension named above; an argument that names none is the same for every part. Nothing has to cross between parts.
All inputs are finite; a program needn't handle non-finite values.
Results may differ from the reference program's by a relative error of at most 0.0025.
Values may be sent and summed in bfloat16 or wider, within the bound.
No kernel may reach another device: no remote copies, remote signals or barrier semaphores. Data moves between devices by JAX's collectives and lax.ppermute only.
A program may use at most 256 MiB of HBM per device.

```python
import math
import jax
import jax.numpy as jnp
from jax import lax

E = 512
NEXT = 32768
ROWS = 8192


def steps_of(own_key, extent, cuts, least, top_value):
    factor_of, own = 1.0, jax.random.fold_in(own_key, 6)
    for dim, blocks in cuts:
        steps = jnp.exp(jax.random.uniform(jax.random.fold_in(own, dim), (blocks,), jnp.float32, least / len(cuts), top_value / len(cuts)))
        factor_of = factor_of * jnp.repeat(steps, extent[dim] // blocks).reshape([-1 if axis == dim else 1 for axis in range(len(extent))])
    return factor_of


def gaussian(rng, extent, deviation, most, shards=(), kind=jnp.bfloat16):
    array = jax.random.normal(rng, extent, jnp.float32) * deviation
    if len(shards) > 0:
        array = steps_of(rng, extent, shards, -0.22, 0.18) * array
    return jnp.clip(array, min=-most, max=most).astype(kind)


def setup_inputs(seed: int = 0, part: int = 0) -> dict:
    key_of = jax.random.split(jax.random.key(seed), 5)
    part_keys = jax.random.split(jax.random.fold_in(key_of[4], part), 5)
    return {
        "grad_table": gaussian(part_keys[0], (ROWS, NEXT), 10.0, 60.0, ((0, 4), (1, 4))),
        "prev_embed": gaussian(key_of[1], (ROWS, E), 1.0, 6.0, ((0, 4), (1, 4))),
        "next_embed": gaussian(key_of[2], (NEXT, E), 1.0, 6.0, ((0, 4), (1, 4))),
        "log_norm": jnp.clip(9.0 + 2.0 * jax.random.uniform(part_keys[3], (ROWS,), jnp.float32) ** steps_of(part_keys[3], (ROWS,), ((0, 4),), -0.2, 0.2), 9.0, 11.0),
    }


def reference(grad_table, prev_embed, next_embed, log_norm):
    scale = 2.0 / math.sqrt(E)
    block = min(512, ROWS)
    count = ROWS // block

    def step(total, index):
        start = (index * block).astype(jnp.int32)
        upstream = lax.dynamic_slice_in_dim(grad_table, start, block, 0)
        left = lax.dynamic_slice_in_dim(prev_embed, start, block, 0)
        norms = lax.dynamic_slice_in_dim(log_norm, start, block, 0)
        logits = scale * jnp.dot(left, next_embed.T, preferred_element_type=jnp.float32)
        probs = jnp.exp(logits - norms[:, None])
        widened = upstream.astype(jnp.float32)
        row_dot = lax.optimization_barrier(jnp.sum(widened * probs, axis=1, keepdims=True))
        dlogits = (scale * probs * (widened - row_dot)).astype(jnp.bfloat16)
        prev_part = jnp.dot(dlogits, next_embed, preferred_element_type=jnp.float32)
        total = total + jnp.dot(dlogits.T, left, preferred_element_type=jnp.float32)
        return (total, prev_part)
    initial = jnp.zeros((NEXT, E), jnp.float32)
    next_grad, prev_parts = lax.scan(step, initial, jnp.arange(count, dtype=jnp.int32))
    return (prev_parts.reshape(ROWS, E), next_grad)
```

```python
import functools
import math

import jax
import jax.numpy as jnp
from jax import lax
from jax.experimental import pallas as pl
from jax.experimental.pallas import tpu as pltpu
from jax.sharding import PartitionSpec as P


VMEM_LIMIT = 60 * 2**20
LOG2E = math.log2(math.e)


def xor_swap(x, axis, size, mask):
    return lax.ppermute(x, axis, [(i, i ^ mask) for i in range(size)])


def bits_of(size):
    if size & (size - 1):
        raise ValueError("axis size")
    return [1 << b for b in reversed(range(size.bit_length() - 1))]


def gather_pieces(own, axis, size):
    pieces = [(0, own)]
    for bit in bits_of(size):
        new = []
        for mask, piece in pieces:
            new.append((mask | bit, xor_swap(piece, axis, size, bit)))
        pieces += new
    return pieces


def slots_of(size):
    order = [0]
    for bit in bits_of(size):
        order = order + [mask | bit for mask in order]
    width = size.bit_length() - 1
    return sorted(order, key=lambda m: int(format(m, f"0{width}b")[::-1], 2) if width else 0)


def slot(mask, size):
    width = size.bit_length() - 1
    out = 0
    for b in range(width):
        out = out + ((mask >> b) & 1) * (1 << (width - 1 - b))
    return out


def pass1_kernel(masks_p, masks_n, first, with_t, sub, *refs):
    scal, refs = refs[0], list(refs[1:])
    prev = [refs.pop(0) for _ in masks_p]
    nxt = [refs.pop(0) for _ in masks_n]
    grad, norm = refs.pop(0), refs.pop(0)
    dot_in = None if first[1] else refs.pop(0)
    if not first[0]:
        refs.pop(0)
    table, dot_out = refs.pop(0), refs.pop(0)
    turned = refs.pop(0) if with_t else None
    left, right, acc, norms = refs
    rows, width = table.shape
    step = pl.program_id(0)

    @pl.when(step == 0)
    def _():
        for mask, ref in zip(masks_p, prev):
            w = ref.shape[1]
            at = pl.multiple_of((scal[0] ^ mask) * w, w) if len(masks_p) > 1 else 0
            left[:, pl.ds(at, w)] = ref[...]
        acc[...] = jnp.zeros_like(acc)
        norms[...] = jnp.transpose(jnp.broadcast_to(norm[...] * LOG2E, (128, rows)))
        if with_t:
            turned[...] = jnp.transpose(left[...])

    for mask, ref in zip(masks_n, nxt):
        w = ref.shape[1]
        at = pl.multiple_of((scal[1] ^ mask) * w, w) if len(masks_n) > 1 else 0
        right[:, pl.ds(at, w)] = ref[...]
    scale = 2.0 / math.sqrt(left.shape[1]) * LOG2E
    x = left[...]
    total = acc[...]
    base = norms[...]
    for j in range(width // sub):
        s = slice(j * sub, (j + 1) * sub)
        logits = lax.dot_general(
            x, right[s, :], (((1,), (1,)), ((), ())), preferred_element_type=jnp.float32
        )
        probs = jnp.exp2(scale * logits - jnp.concatenate([base] * (sub // 128), axis=1))
        table[:, s] = probs
        terms = grad[:, s].astype(jnp.float32) * probs
        for t in range(sub // 128):
            total = total + terms[:, t * 128 : (t + 1) * 128]
    acc[...] = total

    @pl.when(step == pl.num_programs(0) - 1)
    def _():
        sums = jnp.sum(jnp.transpose(total), axis=0, keepdims=True)
        dot_out[...] = sums if dot_in is None else sums + dot_in[...]


def pass1(scal, prev, nxt, grad, norm, dot_in, table, start, with_t):
    rows = prev[0][1].shape[0]
    cols = nxt[0][1].shape[0]
    features = sum(p.shape[1] for _, p in prev)
    tile = min(1024, cols)
    off = start // tile
    args = [p for _, p in prev] + [p for _, p in nxt] + [grad, norm]
    specs = [pl.BlockSpec((rows, p.shape[1]), lambda c, s: (0, 0)) for _, p in prev]
    specs += [pl.BlockSpec((tile, p.shape[1]), lambda c, s: (c, 0)) for _, p in nxt]
    specs += [
        pl.BlockSpec((rows, tile), lambda c, s: (0, c + off)),
        pl.BlockSpec((1, rows), lambda c, s: (0, 0)),
    ]
    if dot_in is not None:
        args.append(dot_in)
        specs.append(pl.BlockSpec((1, rows), lambda c, s: (0, 0)))
    alias = {}
    if table is not None:
        alias = {1 + len(args): 0}
        args.append(table)
        specs.append(pl.BlockSpec(memory_space=pl.ANY))
    shapes = [
        jax.ShapeDtypeStruct(grad.shape, jnp.float32),
        jax.ShapeDtypeStruct((1, rows), jnp.float32),
    ]
    outs = [
        pl.BlockSpec((rows, tile), lambda c, s: (0, c + off)),
        pl.BlockSpec((1, rows), lambda c, s: (0, 0)),
    ]
    if with_t:
        shapes.append(jax.ShapeDtypeStruct((features, rows), jnp.bfloat16))
        outs.append(pl.BlockSpec((features, rows), lambda c, s: (0, 0)))
    return pl.pallas_call(
        functools.partial(
            pass1_kernel,
            [m for m, _ in prev],
            [m for m, _ in nxt],
            (table is None, dot_in is None),
            with_t,
            256,
        ),
        grid_spec=pltpu.PrefetchScalarGridSpec(
            num_scalar_prefetch=1,
            grid=(cols // tile,),
            in_specs=specs,
            out_specs=outs,
            scratch_shapes=[
                pltpu.VMEM((rows, features), jnp.bfloat16),
                pltpu.VMEM((tile, features), jnp.bfloat16),
                pltpu.VMEM((rows, 128), jnp.float32),
                pltpu.VMEM((rows, 128), jnp.float32),
            ],
        ),
        out_shape=shapes,
        input_output_aliases=alias,
        cost_estimate=pl.CostEstimate(
            flops=2 * rows * cols * features,
            bytes_accessed=rows * cols * 6,
            transcendentals=rows * cols,
        ),
        compiler_params=pltpu.CompilerParams(
            dimension_semantics=("arbitrary",), vmem_limit_bytes=VMEM_LIMIT
        ),
    )(scal, *args)


def pass2_kernel(masks_n, n_col, n_row, n_dots, modes, sub, *refs):
    add_next, end_next, add_prev, end_prev = modes
    scal, refs = refs[0], list(refs[1:])
    turned = [refs.pop(0) for _ in range(n_row)]
    nxt = [refs.pop(0) for _ in masks_n]
    grad, table = refs.pop(0), refs.pop(0)
    dots = [refs.pop(0) for _ in range(n_dots)]
    refs.pop(0)
    next_in = refs.pop(0) if add_next else None
    prev_in = refs.pop(0) if add_prev else None
    token = refs.pop(0)
    next_out = [refs.pop(0) for _ in range(1 + end_next)]
    prev_out = [refs.pop(0) for _ in range(1 + end_prev)]
    right, dot_cols = refs[0], refs[1]
    acc = refs[2] if end_prev else prev_out[0]
    rows, width = table.shape
    step = pl.program_id(0)
    features = right.shape[1]
    half = features // 2

    @pl.when(step == 0)
    def _():
        row = dots[0][...]
        for ref in dots[1:]:
            row = row + ref[...]
        dot_cols[...] = jnp.transpose(jnp.broadcast_to(row, (128, rows)))
        acc[...] = prev_in[...] if add_prev else jnp.zeros_like(acc)
        token[...] = jnp.zeros_like(token)

    for mask, ref in zip(masks_n, nxt):
        w = ref.shape[1]
        at = 0
        if len(masks_n) > 1:
            at = pl.multiple_of(slot((scal[1] ^ mask) ^ scal[0], n_col) * w, w)
        right[:, pl.ds(at, w)] = ref[...]
    scale = 2.0 / math.sqrt(features)
    left = jnp.concatenate([ref[...] for ref in turned], axis=0)
    base = dot_cols[...]
    total = None
    for j in range(width // sub):
        s = slice(j * sub, (j + 1) * sub)
        wide = grad[:, s].astype(jnp.float32)
        shift = jnp.concatenate([base] * (sub // 128), axis=1)
        d = ((scale * table[:, s]) * (wide - shift)).astype(jnp.bfloat16)
        t = jnp.dot(left, d, preferred_element_type=jnp.float32)
        if add_next:
            t = t + next_in[:, s]
        if end_next:
            next_out[0][:, s] = t[:half]
            next_out[1][:, s] = t[half:].astype(jnp.bfloat16)
        else:
            next_out[0][:, s] = t
        q = jnp.dot(d, right[s, :], preferred_element_type=jnp.float32)
        total = q if total is None else total + q
    acc[...] += total

    if end_prev:

        @pl.when(step == pl.num_programs(0) - 1)
        def _():
            prev_out[0][...] = acc[:, :half]
            prev_out[1][...] = acc[:, half:].astype(jnp.bfloat16)


def pass2(scal, turned, nxt, grad, table, dots, token, next_in, prev_in, row0, rows, start, cols,
          piece_start, n_col, n_row, end_next, end_prev):
    features = turned.shape[0]
    tile = min(1024, cols)
    off, poff, rb = start // tile, (start - piece_start) // tile, row0 // rows
    order = slots_of(n_row)
    w = features // n_row
    once = pl.Buffered(1)
    args = [turned] * n_row + [p for _, p in nxt] + [grad, table, *dots, token]
    specs = [
        pl.BlockSpec((w, rows), lambda c, s, m=m: (s[1] ^ m, rb), pipeline_mode=once)
        for m in order
    ]
    specs += [pl.BlockSpec((tile, p.shape[1]), lambda c, s: (c + poff, 0)) for _, p in nxt]
    specs += [pl.BlockSpec((rows, tile), lambda c, s: (rb, c + off))] * 2
    specs += [pl.BlockSpec((1, rows), lambda c, s: (0, rb)) for _ in dots]
    specs += [pl.BlockSpec(memory_space=pl.ANY)]
    if next_in is not None:
        args.append(next_in)
        specs.append(pl.BlockSpec((features, tile), lambda c, s: (0, c)))
    if prev_in is not None:
        pb = 0 if prev_in.shape[0] == rows else rb
        args.append(prev_in)
        specs.append(pl.BlockSpec((rows, features), lambda c, s: (pb, 0), pipeline_mode=once))
    half = features // 2
    f32, bf16 = jnp.float32, jnp.bfloat16
    shapes = [jax.ShapeDtypeStruct((8, 128), f32)]
    outs = [pl.BlockSpec((8, 128), lambda c, s: (0, 0))]
    kinds = [(half, f32), (half, bf16)] if end_next else [(features, f32)]
    for h, kind in kinds:
        shapes.append(jax.ShapeDtypeStruct((h, cols), kind))
        outs.append(pl.BlockSpec((h, tile), lambda c, s: (0, c)))
    kinds = [(half, f32), (half, bf16)] if end_prev else [(features, f32)]
    for h, kind in kinds:
        shapes.append(jax.ShapeDtypeStruct((rows, h), kind))
        outs.append(pl.BlockSpec((rows, h), lambda c, s: (0, 0)))
    scratch = [pltpu.VMEM((tile, features), bf16), pltpu.VMEM((rows, 128), f32)]
    if end_prev:
        scratch.append(pltpu.VMEM((rows, features), f32))
    out = pl.pallas_call(
        functools.partial(
            pass2_kernel,
            [m for m, _ in nxt],
            n_col,
            n_row,
            len(dots),
            (next_in is not None, end_next, prev_in is not None, end_prev),
            min(512, tile),
        ),
        grid_spec=pltpu.PrefetchScalarGridSpec(
            num_scalar_prefetch=1,
            grid=(cols // tile,),
            in_specs=specs,
            out_specs=outs,
            scratch_shapes=scratch,
        ),
        out_shape=shapes,
        cost_estimate=pl.CostEstimate(
            flops=4 * rows * cols * features, bytes_accessed=rows * cols * 6, transcendentals=0
        ),
        compiler_params=pltpu.CompilerParams(
            dimension_semantics=("arbitrary",), vmem_limit_bytes=VMEM_LIMIT
        ),
    )(scal, *args)
    split = 2 + end_next
    return out[0], tuple(out[1:split]), tuple(out[split:])


def turn_kernel(keep, got, *refs):
    refs[-1][...] = jnp.transpose(keep[...] + got[...].astype(jnp.float32))


def turn_into(out, keep, got, start, cols):
    w, width = keep.shape
    tile = min(1024, width)
    off = start // tile
    args = [keep, got]
    specs = [pl.BlockSpec((w, tile), lambda c: (0, c))] * 2
    alias = {}
    if out is not None:
        args.append(out)
        specs.append(pl.BlockSpec(memory_space=pl.ANY))
        alias = {2: 0}
    return pl.pallas_call(
        turn_kernel,
        grid=(width // tile,),
        in_specs=specs,
        out_specs=pl.BlockSpec((tile, w), lambda c: (c + off, 0)),
        out_shape=jax.ShapeDtypeStruct((cols, w), jnp.float32),
        input_output_aliases=alias,
        cost_estimate=pl.CostEstimate(
            flops=w * width, bytes_accessed=w * width * 10, transcendentals=0
        ),
        compiler_params=pltpu.CompilerParams(dimension_semantics=("arbitrary",)),
    )(*args)


def halve_sums(keep, send, axis, size, dim):
    for bit in reversed(bits_of(size)):
        got = xor_swap(send, axis, size, bit)
        if bit * 2 == size:
            return keep, got
        keep = keep + got.astype(jnp.float32)
        count = keep.shape[dim]
        send = lax.slice_in_dim(keep, count // 2, count, axis=dim).astype(jnp.bfloat16)
        keep = lax.slice_in_dim(keep, 0, count // 2, axis=dim)


def assembled(pieces, index):
    where = sorted(range(len(pieces)), key=lambda i: pieces[i][0])
    stack = jnp.stack([pieces[i][1] for i in where], axis=1)
    out = jnp.take(stack, jnp.arange(len(pieces)) ^ index, axis=1)
    return out.reshape(out.shape[0], -1)


def make_body(n_col, n_row):
    def body(grad, prev_own, next_own, log_norm):
        rows, cols = grad.shape
        z, r = lax.axis_index("col"), lax.axis_index("row")
        scal = jnp.stack([z, r]).astype(jnp.int32)
        norm = log_norm[None, :]
        half, quarter = cols // 2, cols // 4
        placed = prev_own.shape[1] % 128 == 0 and prev_own.shape[1] == next_own.shape[1]

        prev = gather_pieces(prev_own, "col", n_col)
        if not placed:
            prev = [(0, assembled(prev, z))]

        def next_chunk(c):
            own = lax.slice_in_dim(next_own, c * half, (c + 1) * half)
            pieces = gather_pieces(own, "row", n_row)
            if placed:
                return pieces, pieces
            full = assembled(pieces, r)
            blocks = full.reshape(half, n_col, -1)
            order = jnp.array(slots_of(n_col)) ^ z
            return [(0, full)], [(0, jnp.take(blocks, order, axis=1).reshape(full.shape))]

        chunks = [next_chunk(c) for c in range(2)]
        table, dot, turned = pass1(
            scal, prev, chunks[0][0], grad, norm, None, None, 0, True
        )
        table, dot = pass1(scal, prev, chunks[1][0], grad, norm, dot, table, half, False)
        if n_col <= 4:
            dots = [dot] + [xor_swap(dot, "col", n_col, m) for m in range(1, n_col)]
        else:
            dots = [lax.psum(dot, "col")]

        token = jnp.zeros((8, 128), jnp.float32)
        mid = rows // 2
        last = half + quarter
        plan = [
            (0, rows, 0, half),
            (0, rows, half, quarter),
            (0, mid, last, quarter),
            (mid, mid, last, quarter),
        ]
        prev_sum, next_part, next_done, prev_done = None, None, {}, []
        for row0, height, start, width in plan:
            c = start // half
            end_prev, end_next = height < rows, row0 + height == rows
            token, n_out, p_out = pass2(
                scal, turned, chunks[c][1], grad, table, dots, token, next_part, prev_sum,
                row0, height, start, width, c * half, n_col, n_row, end_next, end_prev,
            )
            if end_next:
                next_done[start] = halve_sums(*n_out, "row", n_row, 0)
            else:
                next_part = n_out[0]
            if end_prev:
                prev_done.append(halve_sums(*p_out, "col", n_col, 1))
            else:
                prev_sum = p_out[0]
        next_grad = None
        for start in sorted(next_done):
            next_grad = turn_into(next_grad, *next_done[start], start, cols)
        prev_grad = jnp.concatenate([k + g.astype(jnp.float32) for k, g in prev_done], axis=0)
        return (prev_grad, next_grad)

    return body


def solution(mesh):
    placed = (P(("parts", "row"), "col"), P("row", "col"), P("col", "row"), P(("parts", "row")))
    n_col, n_row = mesh.shape["col"], mesh.shape["row"]
    return jax.shard_map(
        make_body(n_col, n_row),
        mesh=mesh,
        in_specs=placed,
        out_specs=(P(("parts", "row"), "col"), P(("parts", "col"), "row")),
        check_vma=False,
    )
```

```python
import functools
import math

import jax
import jax.numpy as jnp
from jax import lax
from jax.experimental import pallas as pl
from jax.experimental.pallas import tpu as pltpu
from jax.sharding import PartitionSpec as P


MIB = 2**20
CUT, LAST = 3, 2
TILE = 512
LIMIT2 = 36
LOG2E = math.log2(math.e)


def xor_swap(x, axis, size, mask):
    return lax.ppermute(x, axis, [(i, i ^ mask) for i in range(size)])


def bits_of(size):
    if size & (size - 1):
        raise ValueError("axis size")
    return [1 << b for b in reversed(range(size.bit_length() - 1))]


def gather_pieces(own, axis, size, direct=False):
    pieces = [(0, own)]
    if direct and size <= 4:
        for mask in range(1, size):
            pieces.append((mask, xor_swap(own, axis, size, mask)))
        return pieces
    for bit in bits_of(size):
        new = []
        for mask, piece in pieces:
            new.append((mask | bit, xor_swap(piece, axis, size, bit)))
        pieces += new
    return pieces


def slots_of(size):
    order = [0]
    for bit in bits_of(size):
        order = order + [mask | bit for mask in order]
    width = size.bit_length() - 1
    return sorted(order, key=lambda m: int(format(m, f"0{width}b")[::-1], 2) if width else 0)


def tile_for(cap, *sizes):
    while any(n % cap for n in sizes):
        cap //= 2
    return cap


def slot(mask, size):
    width = size.bit_length() - 1
    out = 0
    for b in range(width):
        out = out + ((mask >> b) & 1) * (1 << (width - 1 - b))
    return out


def pass1_kernel(where_p, masks_n, counts, sub, *refs):
    n_alias, add_dot, with_t = counts
    scal, refs = refs[0], list(refs[1:])
    prev = [refs.pop(0) for _ in where_p]
    nxt = [refs.pop(0) for _ in masks_n]
    grad, norm = refs.pop(0), refs.pop(0)
    dot_in = refs.pop(0) if add_dot else None
    del refs[:n_alias]
    table, dot_out = refs.pop(0), refs.pop(0)
    turned = refs.pop(0) if with_t else None
    left, right, acc, norms = refs
    rows, width = table.shape
    step = pl.program_id(0)

    @pl.when(step == 0)
    def _():
        for (mask, row0), ref in zip(where_p, prev):
            h, w = ref.shape
            at = 0 if w == left.shape[1] else pl.multiple_of((scal[0] ^ mask) * w, w)
            left[row0 : row0 + h, pl.ds(at, w)] = ref[...]
        acc[...] = jnp.zeros_like(acc)
        norms[...] = jnp.transpose(jnp.broadcast_to(norm[...] * LOG2E, (128, rows)))
        if with_t:
            turned[...] = jnp.transpose(left[...])

    for mask, ref in zip(masks_n, nxt):
        w = ref.shape[1]
        at = 0 if w == right.shape[1] else pl.multiple_of((scal[1] ^ mask) * w, w)
        right[:, pl.ds(at, w)] = ref[...]
    scale = 2.0 / math.sqrt(left.shape[1]) * LOG2E
    x = left[...]
    total = acc[...]
    base = norms[...]
    for j in range(width // sub):
        s = slice(j * sub, (j + 1) * sub)
        logits = lax.dot_general(
            x, right[s, :], (((1,), (1,)), ((), ())), preferred_element_type=jnp.float32
        )
        probs = jnp.exp2(scale * logits - jnp.concatenate([base] * (sub // 128), axis=1))
        table[:, s] = probs
        terms = grad[:, s].astype(jnp.float32) * probs
        for t in range(sub // 128):
            total = total + terms[:, t * 128 : (t + 1) * 128]
    acc[...] = total

    @pl.when(step == pl.num_programs(0) - 1)
    def _():
        sums = jnp.sum(jnp.transpose(total), axis=0, keepdims=True)
        dot_out[...] = sums if dot_in is None else sums + dot_in[...]


def pass1(scal, prev, nxt, grad, norm, dot, table, turned, row0, rows, start, first):
    all_rows = grad.shape[0]
    cols = nxt[0][1].shape[0]
    features = sum(p.shape[1] for _, p in nxt)
    tile = tile_for(1024, cols, start)
    off, rb = start // tile, row0 // rows
    row_spec = pl.BlockSpec((1, rows), lambda c, s: (0, rb))
    turn_spec = pl.BlockSpec((features, rows), lambda c, s: (0, rb))
    window = pl.BlockSpec((rows, tile), lambda c, s: (rb, c + off))
    args = [p for _, _, p in prev] + [p for _, p in nxt] + [grad, norm]
    specs = [
        pl.BlockSpec(p.shape, lambda c, s: (0, 0), pipeline_mode=pl.Buffered(1))
        for _, _, p in prev
    ]
    specs += [pl.BlockSpec((tile, p.shape[1]), lambda c, s: (c, 0)) for _, p in nxt]
    specs += [window, row_spec]
    if not first:
        args.append(dot)
        specs.append(row_spec)
    shapes = [
        jax.ShapeDtypeStruct(grad.shape, jnp.float32),
        jax.ShapeDtypeStruct((1, all_rows), jnp.float32),
    ]
    outs = [window, row_spec]
    kept = [(table, 0)]
    if first:
        shapes.append(jax.ShapeDtypeStruct((features, all_rows), jnp.bfloat16))
        outs.append(turn_spec)
        kept += [(dot, 1), (turned, 2)]
    alias = {}
    for array, place in kept:
        if array is not None:
            alias[1 + len(args)] = place
            args.append(array)
            specs.append(pl.BlockSpec(memory_space=pl.ANY))
    return pl.pallas_call(
        functools.partial(
            pass1_kernel,
            [(m, r) for m, r, _ in prev],
            [m for m, _ in nxt],
            (len(alias), not first, first),
            min(256, tile),
        ),
        grid_spec=pltpu.PrefetchScalarGridSpec(
            num_scalar_prefetch=1,
            grid=(cols // tile,),
            in_specs=specs,
            out_specs=outs,
            scratch_shapes=[
                pltpu.VMEM((rows, features), jnp.bfloat16),
                pltpu.VMEM((tile, features), jnp.bfloat16),
                pltpu.VMEM((rows, 128), jnp.float32),
                pltpu.VMEM((rows, 128), jnp.float32),
            ],
        ),
        out_shape=shapes,
        input_output_aliases=alias,
        cost_estimate=pl.CostEstimate(
            flops=2 * rows * cols * features,
            bytes_accessed=rows * cols * 6,
            transcendentals=rows * cols,
        ),
        compiler_params=pltpu.CompilerParams(
            dimension_semantics=("arbitrary",), vmem_limit_bytes=(36 if rows == all_rows else 24) * MIB
        ),
    )(scal, *args)


def cuts_of(size):
    cuts, hi = [(0, 1)], 1
    while hi < size:
        cuts.append((hi, 2 * hi))
        hi *= 2
    return cuts


def pass2_kernel(masks_n, n_col, n_row, n_dots, add_prev, windows, halves, sub, *refs):
    scal, refs = refs[0], list(refs[1:])
    turned = [refs.pop(0) for _ in range(n_row)]
    nxt = [refs.pop(0) for _ in masks_n]
    grad, table = refs.pop(0), refs.pop(0)
    dots = [refs.pop(0) for _ in range(n_dots)]
    prev_in = refs.pop(0) if add_prev else None
    next_out = [[refs.pop(0) for _ in cuts] for _, _, cuts in windows]
    prev_out = [[refs.pop(0) for _ in cuts] for _, _, cuts in halves]
    right, dot_cols = refs[0], refs[1]
    acc = refs[2] if len(refs) > 2 else prev_out[0][0]
    rows, width = table.shape
    step = pl.program_id(0)
    features = right.shape[1]

    @pl.when(step == 0)
    def _():
        row = dots[0][...]
        for ref in dots[1:]:
            row = row + ref[...]
        dot_cols[...] = jnp.transpose(jnp.broadcast_to(row, (128, rows)))
        acc[...] = prev_in[...] if add_prev else jnp.zeros_like(acc)

    for mask, ref in zip(masks_n, nxt):
        w = ref.shape[1]
        at = 0
        if w < features:
            at = pl.multiple_of(slot((scal[1] ^ mask) ^ scal[0], n_col) * w, w)
        right[:, pl.ds(at, w)] = ref[...]
    scale = 2.0 / math.sqrt(features)
    left = jnp.concatenate([ref[...] for ref in turned], axis=0)
    base = dot_cols[...]
    total = None
    for j in range(width // sub):
        s = slice(j * sub, (j + 1) * sub)
        wide = grad[:, s].astype(jnp.float32)
        shift = jnp.concatenate([base] * (sub // 128), axis=1)
        d = ((scale * table[:, s]) * (wide - shift)).astype(jnp.bfloat16)
        t = jnp.dot(left, d, preferred_element_type=jnp.float32)
        for (lo, hi, cuts), outs in zip(windows, next_out):

            @pl.when((step >= lo) & (step < hi))
            def _(cuts=cuts, outs=outs):
                for ref, (top, end) in zip(outs, cuts):
                    ref[:, s] = t[top:end].astype(ref.dtype)

        q = jnp.dot(d, right[s, :], preferred_element_type=jnp.float32)
        total = q if total is None else total + q
    acc[...] += total

    if len(refs) > 2:

        @pl.when(step == pl.num_programs(0) - 1)
        def _():
            for (lo, hi, cuts), outs in zip(halves, prev_out):
                for ref, (top, end) in zip(outs, cuts):
                    ref[...] = acc[lo:hi, top:end].astype(ref.dtype)


def cuts_of(size, features, direct=False):
    f32, bf16 = jnp.float32, jnp.bfloat16
    cuts, hi = [(0, 1, f32)], 1
    while hi < size:
        if direct:
            cuts += [(hi + i, hi + i + 1, bf16) for i in range(hi)]
        else:
            cuts.append((hi, 2 * hi, bf16 if 2 * hi == size else f32))
        hi *= 2
    w = features // size
    return [(lo * w, hi * w, kind) for lo, hi, kind in cuts]


def pass2(scal, turned, nxt, grad, table, dots, prev_in, start, windows, last, n_col, n_row):
    features, rows = turned.shape
    cols = nxt[0][1].shape[0]
    tile = tile_for(TILE, cols, start, *(w for w, _ in windows))
    off = start // tile
    order = slots_of(n_row)
    w = features // n_row
    once = pl.Buffered(1)
    f32, bf16 = jnp.float32, jnp.bfloat16
    args = [turned] * n_row + [p for _, p in nxt] + [grad, table, *dots]
    specs = [
        pl.BlockSpec((w, rows), lambda c, s, m=m: (s[1] ^ m, 0), pipeline_mode=once) for m in order
    ]
    specs += [pl.BlockSpec((tile, p.shape[1]), lambda c, s: (c, 0)) for _, p in nxt]
    specs += [pl.BlockSpec((rows, tile), lambda c, s: (0, c + off))] * 2
    specs += [pl.BlockSpec((1, rows), lambda c, s: (0, 0)) for _ in dots]
    if prev_in is not None:
        args.append(prev_in)
        specs.append(pl.BlockSpec((rows, features), lambda c, s: (0, 0), pipeline_mode=once))
    shapes, outs, steps, lo = [], [], [], 0
    for width, direct in windows:
        size = width // tile
        cuts = cuts_of(n_row, features, direct)
        steps.append((lo, lo + size, [c[:2] for c in cuts]))
        for top, end, kind in cuts:
            shapes.append(jax.ShapeDtypeStruct((end - top, width), kind))
            outs.append(
                pl.BlockSpec(
                    (end - top, tile),
                    lambda c, s, lo=lo, size=size: (0, jnp.clip(c - lo, 0, size - 1)),
                )
            )
        lo += size
    scratch = [pltpu.VMEM((tile, features), bf16), pltpu.VMEM((rows, 128), f32)]
    halves = [(0, rows, [(0, features, f32)])]
    if last:
        scratch.append(pltpu.VMEM((rows, features), f32))
        halves = [
            (0, rows // 2, cuts_of(n_col, features, n_col <= 4)),
            (rows // 2, rows, cuts_of(n_col, features)),
        ]
    for top, end, cuts in halves:
        for a, b, kind in cuts:
            shapes.append(jax.ShapeDtypeStruct((end - top, b - a), kind))
            outs.append(pl.BlockSpec((end - top, b - a), lambda c, s: (0, 0)))
    halves = [(top, end, [c[:2] for c in cuts]) for top, end, cuts in halves]
    out = pl.pallas_call(
        functools.partial(
            pass2_kernel,
            [m for m, _ in nxt],
            n_col,
            n_row,
            len(dots),
            prev_in is not None,
            steps,
            halves,
            min(512, tile),
        ),
        grid_spec=pltpu.PrefetchScalarGridSpec(
            num_scalar_prefetch=1,
            grid=(cols // tile,),
            in_specs=specs,
            out_specs=outs,
            scratch_shapes=scratch,
        ),
        out_shape=shapes,
        cost_estimate=pl.CostEstimate(
            flops=4 * rows * cols * features, bytes_accessed=rows * cols * 6, transcendentals=0
        ),
        compiler_params=pltpu.CompilerParams(
            dimension_semantics=("arbitrary",), vmem_limit_bytes=LIMIT2 * MIB
        ),
    )(scal, *args)
    out = list(out)
    return [[[out.pop(0) for _ in cuts] for _, _, cuts in group] for group in (steps, halves)]


def turn_kernel(n_terms, *refs):
    total = refs[0][...]
    for ref in refs[1:n_terms]:
        total = total + ref[...].astype(jnp.float32)
    refs[-1][...] = jnp.transpose(total)


def turn_into(out, terms, start, cols):
    w, width = terms[0].shape
    tile = tile_for(1024, width, start)
    off = start // tile
    args = list(terms)
    specs = [pl.BlockSpec((w, tile), lambda c: (0, c))] * len(terms)
    alias = {}
    if out is not None:
        args.append(out)
        specs.append(pl.BlockSpec(memory_space=pl.ANY))
        alias = {len(terms): 0}
    return pl.pallas_call(
        functools.partial(turn_kernel, len(terms)),
        grid=(width // tile,),
        in_specs=specs,
        out_specs=pl.BlockSpec((tile, w), lambda c: (c + off, 0)),
        out_shape=jax.ShapeDtypeStruct((cols, w), jnp.float32),
        input_output_aliases=alias,
        cost_estimate=pl.CostEstimate(
            flops=w * width, bytes_accessed=w * width * 10, transcendentals=0
        ),
        compiler_params=pltpu.CompilerParams(dimension_semantics=("arbitrary",)),
    )(*args)


def halve_sums(parts, axis, size, dim):
    parts = list(parts)
    send, gots = parts.pop(), []
    for bit in reversed(bits_of(size)):
        gots.append(xor_swap(send, axis, size, bit))
        if bit * 2 < size:
            part = parts.pop()
            count = part.shape[dim]
            for got in gots:
                part = part + lax.slice_in_dim(got, count, 2 * count, axis=dim).astype(jnp.float32)
            send = part.astype(jnp.bfloat16)
    return parts + gots


def send_sums(parts, axis, size):
    terms = [parts[0]]
    for mask, part in zip(slots_of(size)[1:], parts[1:]):
        terms.append(xor_swap(part, axis, size, mask))
    return terms


def assembled(pieces, index):
    where = sorted(range(len(pieces)), key=lambda i: pieces[i][0])
    stack = jnp.stack([pieces[i][1] for i in where], axis=1)
    out = jnp.take(stack, jnp.arange(len(pieces)) ^ index, axis=1)
    return out.reshape(out.shape[0], -1)


def make_body(n_col, n_row):
    def body(grad, prev_own, next_own, log_norm):
        rows, cols = grad.shape
        z, r = lax.axis_index("col"), lax.axis_index("row")
        scal = jnp.stack([z, r]).astype(jnp.int32)
        norm = log_norm[None, :]
        mid = rows // 2
        cut = cols * CUT // 8
        placed = prev_own.shape[1] % 128 == 0 and prev_own.shape[1] == next_own.shape[1]

        def prev_rows(row0):
            own = lax.slice_in_dim(prev_own, row0, row0 + mid)
            pieces = gather_pieces(own, "col", n_col, row0 > 0)
            return pieces if placed else [(0, assembled(pieces, z))]

        def next_chunk(lo, hi):
            own = lax.slice_in_dim(next_own, lo, hi)
            pieces = gather_pieces(own, "row", n_row)
            if placed:
                return pieces, pieces
            full = assembled(pieces, r)
            blocks = full.reshape(hi - lo, n_col, -1)
            order = jnp.array(slots_of(n_col)) ^ z
            return [(0, full)], [(0, jnp.take(blocks, order, axis=1).reshape(full.shape))]

        prev = [[(m, p) for m, p in prev_rows(row0)] for row0 in (0, mid)]
        chunks = [next_chunk(0, cut), next_chunk(cut, cols)]
        table = dot = turned = None
        for g in range(2):
            table, dot, turned = pass1(
                scal, [(m, 0, p) for m, p in prev[g]], chunks[0][0], grad, norm, dot, table,
                turned, g * mid, mid, 0, True,
            )
        both = [(m, g * mid, p) for g in range(2) for m, p in prev[g]]
        table, dot = pass1(
            scal, both, chunks[1][0], grad, norm, dot, table, None, 0, rows, cut, False
        )
        if n_col <= 4:
            dots = [dot]
            for m in range(1, n_col):
                dots.append(xor_swap(dot, "col", n_col, m))
        else:
            dots = [lax.psum(dot, "col")]

        eighth = cols // 8
        later = (CUT, 8 - CUT - LAST, LAST)
        direct, prev_sum = pass2(
            scal, turned, chunks[0][1], grad, table, dots, None, 0,
            [(later[0] * eighth, True)], False, n_col, n_row,
        )
        halved, sides = pass2(
            scal, turned, chunks[1][1], grad, table, dots, prev_sum[0][0], cut,
            [(later[1] * eighth, False), (later[2] * eighth, False)], True, n_col, n_row,
        )
        next_done = {0: (0, send_sums(direct[0], "row", n_row))}
        for k, parts in enumerate(halved):
            start = sum(later[: k + 1]) * eighth
            next_done[start] = (k + 1, halve_sums(parts, "row", n_row, 0))
        if n_col <= 4:
            prev_done = [send_sums(sides[0], "col", n_col)]
        else:
            prev_done = [halve_sums(sides[0], "col", n_col, 1)]
        prev_done.append(halve_sums(sides[1], "col", n_col, 1))
        next_grad = None
        for start in sorted(next_done):
            k, terms = next_done[start]
            next_grad = turn_into(next_grad, terms, start, cols)
        sides = []
        for k, terms in enumerate(prev_done):
            w = terms[0].shape[1]
            sides.append(sum(t[:, :w].astype(jnp.float32) for t in terms))
        return (jnp.concatenate(sides, axis=0), next_grad)

    return body


def solution(mesh):
    placed = (P(("parts", "row"), "col"), P("row", "col"), P("col", "row"), P(("parts", "row")))
    return jax.shard_map(
        make_body(mesh.shape["col"], mesh.shape["row"]),
        mesh=mesh,
        in_specs=placed,
        out_specs=(P(("parts", "row"), "col"), P(("parts", "col"), "row")),
        check_vma=False,
    )
```
